128 devices in a mesh: rows: 16 (over z, x), feat: 8 (over y, core).
Axes of the slice: x: 4, y: 4, z: 4, core: 2. Of those that a mesh axis runs over, the one named last changes fastest.
Arguments:
- scores: float32 [524288, 64], P(('rows', 'feat'))
- labels: int32 [524288], P('rows'), may hold values from 0 to 63
- bins: int32 [256, 524288], P('feat', 'rows'), may hold values from 0 to 63
- elected: int32 [64, 32], P(None, 'feat'), may hold values from 0 to 255, as said below
Outputs:
- gains: float32 [64, 32, 63], P('rows', 'feat')
The draws below stay inside these ranges and needn't reach their ends.
Inputs may be any that keep to these rules, and one draw needn't show every extreme that they name: `elected`: for every class and every j < 8, columns j * 4 to (j + 1) * 4 - 1 hold 4 distinct features of the range j * 32 to (j + 1) * 32 - 1.
All inputs are finite; a program needn't handle non-finite values.
Results may differ from the reference program's by a relative error of at most 0.0026.
Values may be sent and summed in bfloat16 or wider, within the bound.
A program may use at most 64 MiB of HBM per device.

```python
import jax
import jax.numpy as jnp
from jax import lax

C = 64
F = 256
BINS = 64
EPG = 4
ROWS = 524288
FGRP = 32
ELECT = 32


def common_bins(key):
    return jax.random.randint(jax.random.fold_in(key, 11), (F, ROWS), 0, BINS, jnp.int32)


def common_elected(key):
    group_count = F // FGRP
    keys = jax.random.split(jax.random.fold_in(key, 12), C * group_count)
    picks = jax.vmap(lambda sub_key: jax.random.permutation(sub_key, FGRP)[:EPG])(keys)
    picks = picks.reshape(C, group_count, EPG).astype(jnp.int32)
    starts = (jnp.arange(group_count, dtype=jnp.int32) * FGRP)[None, :, None]
    return (picks + starts).reshape(C, ELECT).astype(jnp.int32)


def draw_bins(key, part):
    return common_bins(key)


def draw_elected(key, part):
    return common_elected(key)


def draw_scores(key, part):
    bin_table = common_bins(key)
    chosen = common_elected(key)
    first_bins = bin_table[chosen[:, 0], :]
    last_bins = bin_table[chosen[:, ELECT - 1], :]
    ramp = (first_bins + last_bins).astype(jnp.float32).T / (2.0 * (BINS - 1))
    spread = 0.4 + 2.4 * ramp
    key_a = jax.random.fold_in(jax.random.fold_in(key, 13), 0)
    base = jax.random.normal(key_a, (ROWS, C), jnp.float32)
    return spread * base - 0.5 * spread * spread


def place_ends(drawn, own_key, low, high):
    spot = [jax.random.randint(jax.random.fold_in(own_key, axis), (), 0, length) for axis, length in enumerate(drawn.shape)]
    widest = drawn.shape.index(max(drawn.shape))
    next_to = spot[:widest] + [(spot[widest] + 1) % drawn.shape[widest]] + spot[widest + 1:]
    return drawn.at[tuple(spot)].set(low).at[tuple(next_to)].set(high)


def setup_inputs(seed: int = 0) -> dict:
    key_list = jax.random.split(jax.random.key(seed), 5)
    return {
        "scores": draw_scores(jax.random.fold_in(key_list[4], 71), 0),
        "labels": place_ends(jax.random.randint(key_list[1], (ROWS,), 0, C), jax.random.fold_in(key_list[1], 1), 0, C - 1).astype(jnp.int32),
        "bins": draw_bins(jax.random.fold_in(key_list[4], 71), 0),
        "elected": draw_elected(jax.random.fold_in(key_list[4], 71), 0),
    }


l2_penalty = 1.0


def grad_columns(scores, labels):
    row_max = jnp.max(scores, axis=1, keepdims=True)
    expon = jnp.exp(scores - row_max)
    probs = expon / jnp.sum(expon, axis=1, keepdims=True)
    target = (labels[:, None] == jnp.arange(scores.shape[1], dtype=jnp.int32)[None, :]).astype(jnp.float32)
    grad = (probs - target).astype(jnp.bfloat16)
    hess = (probs * (1.0 - probs)).astype(jnp.bfloat16)
    return grad, hess


def split_gains(hist):
    left_g = jnp.cumsum(hist[..., 0], axis=-1)
    left_h = jnp.cumsum(hist[..., 1], axis=-1)
    tot_g = left_g[..., -1:]
    tot_h = left_h[..., -1:]
    right_g = tot_g - left_g
    right_h = tot_h - left_h
    split_gain = 0.5 * (left_g * left_g / (left_h + l2_penalty) + right_g * right_g / (right_h + l2_penalty) - tot_g * tot_g / (tot_h + l2_penalty))
    return split_gain[..., :-1]


def reference(scores, labels, bins, elected):
    grad, hess = grad_columns(scores, labels)
    grad_t = grad.astype(jnp.float32).T
    hess_t = hess.astype(jnp.float32).T
    n_elect = elected.shape[1]
    n_rows = scores.shape[0]
    offsets = (jnp.arange(n_elect, dtype=jnp.int32) * BINS)[:, None]

    def per_class(packed):
        chosen, gcol, hcol = packed
        index_all = (bins[chosen, :] + offsets).reshape(-1)
        gsum = jax.ops.segment_sum(jnp.broadcast_to(gcol[None, :], (n_elect, n_rows)).reshape(-1), index_all, num_segments=n_elect * BINS)
        hsum = jax.ops.segment_sum(jnp.broadcast_to(hcol[None, :], (n_elect, n_rows)).reshape(-1), index_all, num_segments=n_elect * BINS)
        return jnp.stack([gsum.reshape(n_elect, BINS), hsum.reshape(n_elect, BINS)], axis=-1)

    hist = lax.map(per_class, (elected, grad_t, hess_t))
    return split_gains(hist)
```

```python
import functools

import jax
import jax.numpy as jnp
from jax import lax
from jax.experimental import pallas as pl
from jax.experimental.pallas import tpu as pltpu
from jax.sharding import PartitionSpec as P

BINS = 64
LANES = 128
GROUP = 4
BLOCK = 256
MESH = pl.DeviceIdType.MESH
bf16 = jnp.bfloat16
f8 = jnp.float8_e4m3fn
f32 = jnp.float32

l2_penalty = 1.0


def code_probs(scores):
    expon = jnp.exp(scores - jnp.max(scores, axis=0, keepdims=True))
    probs = expon * (1.0 / jnp.sum(expon, axis=0, keepdims=True))
    return jnp.where(probs > 0.5, jnp.minimum(probs - 1.0, -1e-30), probs).astype(bf16)


def grad_hess(coded, is_label):
    zero, one = jnp.zeros((), bf16), jnp.ones((), bf16)
    shift = jnp.where(coded < zero, one, zero) - jnp.where(is_label, one, zero)
    size = jnp.abs(coded)
    return coded + shift, size * (one - size)


def kernel(
    n_rows,
    n_feat,
    scores_hbm,
    labels_ref,
    bins_hbm,
    elected_ref,
    out_ref,
    scores,
    bins,
    coded,
    gh,
    acc,
    sbuf,
    rbuf,
    in_sem,
    bins_sem,
    send_sem,
    recv_sem,
    send2_sem,
    recv2_sem,
):
    n_y = n_feat // 2
    row = lax.axis_index("rows")
    feat = lax.axis_index("feat")
    y, core = feat // 2, feat % 2
    other = y * 2 + 1 - core
    plus = lax.rem(y + 1, n_y) * 2 + core
    minus = lax.rem(y + n_y - 1, n_y) * 2 + core
    sub = coded.shape[3]
    classes = coded.shape[2]
    fgrp = bins.shape[1]

    barrier = pltpu.get_barrier_semaphore()
    for peer in (other, plus, minus):
        pl.semaphore_signal(barrier, inc=1, device_id=(row, peer), device_id_type=MESH)
    for dist in range(1, n_rows):
        peer = lax.rem(row + dist, n_rows)
        pl.semaphore_signal(barrier, inc=1, device_id=(peer, feat), device_id_type=MESH)

    def source(stage, kind):
        back = jnp.where(stage == 0, 0, jnp.where(stage == 3, 2, 1))
        side = lax.rem(kind, 2)
        from_y = lax.rem(jnp.where(side == 0, y + n_y - back, y + back), n_y)
        from_core = jnp.where(kind < 2, core, 1 - core)
        half_a = jnp.where(stage == 2, 1, 0)
        half = jnp.where(side == 0, half_a, 1 - half_a)
        return from_y * 2 + from_core, half

    def bins_copy(stage, kind):
        src, half = source(stage, kind)
        start = pl.multiple_of((src * 2 + half) * sub, sub)
        slot = stage * 4 + kind
        return pltpu.make_async_copy(
            bins_hbm.at[:, pl.ds(start, sub)], bins.at[slot], bins_sem.at[slot]
        )

    copies = [
        pltpu.make_async_copy(
            scores_hbm.at[:, pl.ds(half * sub, sub)], scores.at[half], in_sem.at[half]
        )
        for half in range(2)
    ]
    for copy in copies:
        copy.start()
    for stage in range(4):
        for kind in range(4):
            bins_copy(stage, kind).start()

    for half in range(2):
        copies[half].wait()
        for lane in range(0, sub, BLOCK):
            coded[feat, half, :, lane : lane + BLOCK] = code_probs(
                scores[half, :, lane : lane + BLOCK]
            )

    pl.semaphore_wait(barrier, n_rows + 2)

    def send(src, half, peer, send_slot, recv_slot):
        return pltpu.make_async_remote_copy(
            src_ref=coded.at[src, half],
            dst_ref=coded.at[src, half],
            send_sem=send_sem.at[send_slot],
            recv_sem=recv_sem.at[recv_slot],
            device_id=(row, peer),
            device_id_type=MESH,
        )

    send(feat, 0, plus, 0, 4).start()
    send(feat, 1, minus, 1, 5).start()
    send(feat, 0, other, 2, 2).start()
    send(feat, 1, other, 3, 3).start()
    send(feat, 1, plus, 4, 8).start()
    send(feat, 0, minus, 5, 9).start()

    acc[...] = jnp.zeros_like(acc)

    class_ids = lax.broadcasted_iota(jnp.int32, (classes, LANES), 0).astype(f32).astype(bf16)

    def piece(index, carry):
        stage, kind = index // 4, lax.rem(index, 4)
        src, half = source(stage, kind)

        @pl.when((stage > 0) | (kind > 1))
        def _():
            send(src, half, other, 0, index).wait_recv()

        @pl.when((stage > 0) & (kind < 2))
        def _():
            send(src, half, other, 6 + stage * 2 + kind, index + 2).start()

        @pl.when((stage == 1) & (kind < 2))
        def _():
            onward = jnp.where(kind == 0, plus, minus)
            send(src, half, onward, 14 + kind, 12 + kind).start()

        bins_copy(stage, kind).wait()

        tiles = sub // LANES
        first = pl.multiple_of((src * 2 + half) * tiles, tiles)
        for lane in range(0, sub, LANES):
            label = labels_ref[pl.ds(first + lane // LANES, 1), :]
            label = jnp.broadcast_to(label.astype(f32), (classes, LANES)).astype(bf16)
            grad, hess = grad_hess(
                coded[src, half, :, lane : lane + LANES], label == class_ids
            )
            gh[0:classes, lane : lane + LANES] = grad
            gh[classes : 2 * classes, lane : lane + LANES] = hess

        values = gh[...]
        bin_ids = lax.broadcasted_iota(jnp.int32, (BINS, sub), 0).astype(jnp.int8)
        ones, zeros = jnp.ones((BINS, sub), f8), jnp.zeros((BINS, sub), f8)
        for group in range(fgrp // GROUP):
            onehot = []
            for feature in range(group * GROUP, (group + 1) * GROUP):
                code = bins[index, feature : feature + 1, :]
                code = jnp.broadcast_to(code, (BINS, sub)).astype(jnp.int8)
                onehot.append(jnp.where(code == bin_ids, ones, zeros))
            sums = lax.dot_general(
                values,
                jnp.concatenate(onehot, axis=0),
                (((1,), (1,)), ((), ())),
                preferred_element_type=f32,
            )
            columns = slice(group * GROUP * BINS, (group + 1) * GROUP * BINS)
            acc[:, columns] += sums
        return carry

    lax.fori_loop(0, 16, piece, 0)

    n_elect = elected_ref.shape[0]
    local = (elected_ref[...] - feat * fgrp).astype(f32)
    eye = jnp.where(
        lax.broadcasted_iota(jnp.int32, (classes, classes), 0)
        == lax.broadcasted_iota(jnp.int32, (classes, classes), 1),
        1.0,
        0.0,
    ).astype(f32)
    per_class = [
        jnp.sum(eye * local[e : e + 1, :], axis=1, keepdims=True) for e in range(n_elect)
    ]
    lane_ids = lax.broadcasted_iota(jnp.int32, (2 * classes, LANES), 1)
    upper = jnp.where(lane_ids >= BINS, 1.0, 0.0).astype(f32)
    own = classes // n_rows
    for pair in range(n_elect // 2):
        folded = []
        for e in (2 * pair, 2 * pair + 1):
            chosen = jnp.concatenate([per_class[e], per_class[e]], axis=0) - upper
            total = jnp.zeros((2 * classes, LANES), f32)
            for tile in range(fgrp // 2):
                total += jnp.where(
                    chosen == 2.0 * tile, acc[:, tile * LANES : (tile + 1) * LANES], 0.0
                )
            folded.append(total + pltpu.roll(total, BINS, 1))
        picked = jnp.where(lane_ids < BINS, folded[0], folded[1])
        columns = slice(pair * LANES, (pair + 1) * LANES)
        for owner in range(n_rows):
            sbuf[owner, 0:own, columns] = picked[owner * own : (owner + 1) * own]
            sbuf[owner, own : 2 * own, columns] = picked[
                classes + owner * own : classes + (owner + 1) * own
            ]

    def exchange(dist):
        peer = lax.rem(row + dist, n_rows)
        return pltpu.make_async_remote_copy(
            src_ref=sbuf.at[peer],
            dst_ref=rbuf.at[dist],
            send_sem=send2_sem.at[dist],
            recv_sem=recv2_sem.at[dist],
            device_id=(peer, feat),
            device_id_type=MESH,
        )

    for dist in range(1, n_rows):
        exchange(dist).start()
    total = sbuf[row]
    for dist in range(1, n_rows):
        exchange(dist).wait_recv()
        total += rbuf[dist]

    width = n_elect * BINS
    bin_of = lax.rem(lax.broadcasted_iota(jnp.int32, total.shape, 1), BINS)
    left = total
    every = total
    shift = 1
    while shift < BINS:
        left += jnp.where(bin_of >= shift, pltpu.roll(left, shift, 1), 0.0)
        every += jnp.where(
            lax.rem(bin_of, 2 * shift) < shift,
            pltpu.roll(every, width - shift, 1),
            pltpu.roll(every, shift, 1),
        )
        shift *= 2
    right = every - left
    left_g, left_h = left[:own], left[own:]
    right_g, right_h = right[:own], right[own:]
    tot_g, tot_h = every[:own], every[own:]
    gains = 0.5 * (
        left_g * left_g / (left_h + l2_penalty)
        + right_g * right_g / (right_h + l2_penalty)
        - tot_g * tot_g / (tot_h + l2_penalty)
    )
    for e in range(n_elect):
        part = gains[:, (e // 2) * LANES : (e // 2 + 1) * LANES]
        if e % 2:
            part = pltpu.roll(part, BINS, 1)
        for c in range(own):
            out_ref[c, e : e + 1, :] = part[c : c + 1, : BINS - 1]

    send(feat, 0, plus, 0, 4).wait_send()
    send(feat, 1, minus, 1, 5).wait_send()
    send(feat, 0, other, 2, 2).wait_send()
    send(feat, 1, other, 3, 3).wait_send()
    send(feat, 1, plus, 4, 8).wait_send()
    send(feat, 0, minus, 5, 9).wait_send()
    for slot in range(8, 16):
        send(feat, 0, other, slot, 0).wait_send()
    for dist in range(1, n_rows):
        exchange(dist).wait_send()


def shards(scores, labels, bins, elected):
    n_rows, n_feat = lax.axis_size("rows"), lax.axis_size("feat")
    own_rows, classes = scores.shape
    fgrp, rows = bins.shape
    n_elect = elected.shape[1]
    sub = own_rows // 2
    own = classes // n_rows
    dma = pltpu.SemaphoreType.DMA
    return pl.pallas_call(
        functools.partial(kernel, n_rows, n_feat),
        out_shape=jax.ShapeDtypeStruct((own, n_elect, BINS - 1), jnp.float32),
        in_specs=[
            pl.BlockSpec(memory_space=pl.ANY),
            pl.BlockSpec(memory_space=pltpu.VMEM),
            pl.BlockSpec(memory_space=pl.ANY),
            pl.BlockSpec(memory_space=pltpu.VMEM),
        ],
        out_specs=pl.BlockSpec(memory_space=pltpu.VMEM),
        scratch_shapes=[
            pltpu.VMEM((2, classes, sub), f32),
            pltpu.VMEM((16, fgrp, sub), jnp.int32),
            pltpu.VMEM((n_feat, 2, classes, sub), bf16),
            pltpu.VMEM((2 * classes, sub), bf16),
            pltpu.VMEM((2 * classes, fgrp * BINS), f32),
            pltpu.VMEM((n_rows, 2 * own, n_elect * BINS), f32),
            pltpu.VMEM((n_rows, 2 * own, n_elect * BINS), f32),
            dma((2,)),
            dma((16,)),
            dma((16,)),
            dma((16,)),
            dma((n_rows,)),
            dma((n_rows,)),
        ],
        compiler_params=pltpu.CompilerParams(
            collective_id=0, has_side_effects=True, vmem_limit_bytes=48 << 20
        ),
    )(scores.T, labels.reshape(rows // LANES, LANES), bins, elected.T)


def solution(mesh):
    return jax.shard_map(
        shards,
        mesh=mesh,
        in_specs=(P(("rows", "feat"), None), P("rows"), P("feat", "rows"), P(None, "feat")),
        out_specs=P("rows", "feat", None),
        check_vma=False,
    )
```

```python
import functools
import math

import jax
import jax.numpy as jnp
from jax import lax
from jax.experimental import pallas as pl
from jax.experimental.pallas import tpu as pltpu
from jax.sharding import PartitionSpec as P

BINS = 64
LANES = 128
GROUP = 4
PIECES = 32
UNITS = PIECES // 2
X_CHIPS = 4
BLOCK = 256
MESH = pl.DeviceIdType.MESH
bf16 = jnp.bfloat16
f8 = jnp.float8_e4m3fn
f32 = jnp.float32

l2_penalty = 1.0


def code_probs(scores):
    expon = jnp.exp(scores - jnp.max(scores, axis=0, keepdims=True))
    probs = expon * (1.0 / jnp.sum(expon, axis=0, keepdims=True))
    return jnp.where(probs > 0.5, jnp.minimum(probs - 1.0, -1e-30), probs).astype(bf16)


def grad_hess(coded, is_label):
    zero, one = jnp.zeros((), bf16), jnp.ones((), bf16)
    shift = jnp.where(coded < zero, one, zero) - jnp.where(is_label, one, zero)
    size = jnp.abs(coded)
    return coded + shift, size * (one - size)


def kernel(
    n_rows,
    n_x,
    n_feat,
    scores_hbm,
    labels_hbm,
    bins_hbm,
    elected_hbm,
    out_ref,
    scores,
    labels,
    bins,
    elected,
    coded,
    gh,
    acc,
    sbuf,
    rbuf,
    in_sem,
    bins_sem,
    send_sem,
    recv_sem,
    send2_sem,
    recv2_sem,
    all_in,
):
    n_y, n_z = n_feat // 2, n_rows // n_x
    row = lax.axis_index("rows")
    feat = lax.axis_index("feat")
    y, core = feat // 2, feat % 2
    z, x = row // n_x, row % n_x
    other = y * 2 + 1 - core
    plus = lax.rem(y + 1, n_y) * 2 + core
    minus = lax.rem(y + n_y - 1, n_y) * 2 + core
    sub = coded.shape[3]
    classes = coded.shape[2]
    fgrp = bins.shape[1]

    barrier = pltpu.get_barrier_semaphore()
    for peer in (other, plus, minus):
        pl.semaphore_signal(barrier, inc=1, device_id=(row, peer), device_id_type=MESH)
    for dist in range(1, n_x):
        peer = z * n_x + lax.rem(x + dist, n_x)
        pl.semaphore_signal(barrier, inc=1, device_id=(peer, feat), device_id_type=MESH)
    for dist in range(1, n_z):
        peer = lax.rem(z + dist, n_z) * n_x + x
        pl.semaphore_signal(barrier, inc=1, device_id=(peer, feat), device_id_type=MESH)

    def source(index):
        stage, kind = index // 4, lax.rem(index, 4)
        back = jnp.where(stage < 6, 1, 2)
        side = lax.rem(kind, 2)
        from_y = lax.rem(jnp.where(side == 0, y + n_y - back, y + back), n_y)
        from_core = jnp.where(kind < 2, core, 1 - core)
        near = jnp.where(stage == 0, feat, other)
        src = jnp.where(stage < 2, near, from_y * 2 + from_core)
        nth = jnp.where(stage < 2, kind // 2, jnp.where(stage < 6, stage - 2, stage - 6))
        return src, jnp.where(side == 0, nth, 3 - nth)

    def bins_copy(unit, side):
        src, quarter = source(2 * unit + side)
        start = pl.multiple_of((src * 4 + quarter) * sub, sub)
        return pltpu.make_async_copy(
            bins_hbm.at[:, pl.ds(start, sub)],
            bins.at[unit, :, pl.ds(side * sub, sub)],
            bins_sem.at[2 * unit + side],
        )

    own_order = (0, 3, 1, 2)
    copies = [
        pltpu.make_async_copy(
            scores_hbm.at[:, pl.ds(quarter * sub, sub)], scores.at[quarter], in_sem.at[quarter]
        )
        for quarter in own_order
    ]
    small = [
        pltpu.make_async_copy(labels_hbm, labels, in_sem.at[4]),
        pltpu.make_async_copy(elected_hbm, elected, in_sem.at[5]),
    ]
    for copy in copies + small:
        copy.start()

    def start_bins(unit, carry):
        bins_copy(unit, 0).start()
        bins_copy(unit, 1).start()
        return carry

    lax.fori_loop(0, UNITS, start_bins, 0)

    for quarter, copy in zip(own_order, copies):
        copy.wait()
        for lane in range(0, sub, BLOCK):
            lanes = slice(lane, min(lane + BLOCK, sub))
            coded[feat, quarter, :, lanes] = code_probs(scores[quarter, :, lanes])

    def send(src, quarter, peer, send_slot, recv_slot):
        return pltpu.make_async_remote_copy(
            src_ref=coded.at[src, quarter],
            dst_ref=coded.at[src, quarter],
            send_sem=send_sem.at[send_slot],
            recv_sem=recv_sem.at[recv_slot],
            device_id=(row, peer),
            device_id_type=MESH,
        )

    own_sends = []
    for nth in range(4):
        own_sends.append(send(feat, nth, plus, nth, 8 + 4 * nth))
        own_sends.append(send(feat, 3 - nth, minus, 4 + nth, 9 + 4 * nth))
        own_sends.append(send(feat, own_order[nth], other, 8 + nth, 4 + nth))

    acc[...] = jnp.zeros_like(acc)

    class_ids = lax.broadcasted_iota(jnp.int32, (classes, LANES), 0).astype(f32).astype(bf16)

    def receive(unit):
        stage, kind = unit // 2, 2 * lax.rem(unit, 2)
        pieces = [source(2 * unit + side) for side in range(2)]
        for side in range(2):
            send(*pieces[side], other, 0, 2 * unit + side).wait_recv()

        @pl.when((stage > 1) & (kind == 0))
        def _():
            for side in range(2):
                slot = 8 + stage * 2 + side
                send(*pieces[side], other, slot, 2 * unit + side + 2).start()

        @pl.when(((stage == 2) | (stage == 3)) & (kind == 0))
        def _():
            for side, onward in enumerate((plus, minus)):
                slot = 20 + stage * 2 + side
                send(*pieces[side], onward, slot, 2 * unit + side + 16).start()

        for side in range(2):
            bins_copy(unit, side).wait()

    tiles = sub // LANES
    groups = fgrp // GROUP

    def decode(unit):
        for tile in range(2 * tiles):
            src, quarter = source(2 * unit + tile // tiles)
            first = pl.multiple_of((src * 4 + quarter) * tiles, tiles)
            label = labels[pl.ds(first + tile % tiles, 1), :].astype(f32)
            label = jnp.broadcast_to(label, (classes, LANES)).astype(bf16)
            column = tile % tiles * LANES
            grad, hess = grad_hess(
                coded[src, quarter, :, column : column + LANES], label == class_ids
            )
            lanes = slice(tile * LANES, (tile + 1) * LANES)
            gh[0:classes, lanes] = grad
            gh[classes : 2 * classes, lanes] = hess

    def add_unit(unit):
        decode(unit)
        values = gh[...]
        shape = (BINS, 2 * sub)
        bin_ids = lax.broadcasted_iota(jnp.int32, shape, 0).astype(jnp.int8)
        ones, zeros = jnp.ones(shape, f8), jnp.zeros(shape, f8)
        for group in range(groups):
            onehot = []
            for feature in range(group * GROUP, (group + 1) * GROUP):
                code = bins[unit, feature : feature + 1, :]
                code = jnp.broadcast_to(code, shape).astype(jnp.int8)
                onehot.append(jnp.where(code == bin_ids, ones, zeros))
            columns = slice(group * GROUP * BINS, (group + 1) * GROUP * BINS)
            acc[:, columns] += lax.dot_general(
                values,
                jnp.concatenate(onehot, axis=0),
                (((1,), (1,)), ((), ())),
                preferred_element_type=f32,
            )

    for copy in small:
        copy.wait()

    def own_unit(unit):
        bins_copy(unit, 0).wait()
        bins_copy(unit, 1).wait()
        add_unit(unit)

    own_unit(0)
    pl.semaphore_wait(barrier, n_x + n_z + 1)
    for copy in own_sends:
        copy.start()
    for dist in range(1, n_x):
        peer = z * n_x + lax.rem(x + dist, n_x)
        pl.semaphore_signal(all_in, inc=1, device_id=(peer, feat), device_id_type=MESH)
    own_unit(1)

    def next_unit(unit, carry):
        receive(unit)
        add_unit(unit)
        return carry

    lax.fori_loop(2, UNITS, next_unit, 0)

    n_elect = elected.shape[0]
    local = (elected[...] - feat * fgrp).astype(f32)
    eye = jnp.where(
        lax.broadcasted_iota(jnp.int32, (classes, classes), 0)
        == lax.broadcasted_iota(jnp.int32, (classes, classes), 1),
        1.0,
        0.0,
    ).astype(f32)
    per_class = [
        jnp.sum(eye * local[e : e + 1, :], axis=1, keepdims=True) for e in range(n_elect)
    ]
    lane_ids = lax.broadcasted_iota(jnp.int32, (2 * classes, LANES), 1)
    upper = jnp.where(lane_ids >= BINS, 1.0, 0.0).astype(f32)
    own = classes // n_rows
    for pair in range(n_elect // 2):
        folded = []
        for e in (2 * pair, 2 * pair + 1):
            chosen = jnp.concatenate([per_class[e], per_class[e]], axis=0) - upper
            total = jnp.zeros((2 * classes, LANES), f32)
            for tile in range(fgrp // 2):
                total += jnp.where(
                    chosen == 2.0 * tile, acc[:, tile * LANES : (tile + 1) * LANES], 0.0
                )
            folded.append(total + pltpu.roll(total, BINS, 1))
        picked = jnp.where(lane_ids < BINS, folded[0], folded[1])
        columns = slice(pair * LANES, (pair + 1) * LANES)
        for owner in range(n_rows):
            sbuf[owner, 0:own, columns] = picked[owner * own : (owner + 1) * own]
            sbuf[owner, own : 2 * own, columns] = picked[
                classes + owner * own : classes + (owner + 1) * own
            ]

    def exchange(dist):
        peer = lax.rem(row + dist, n_rows)
        return pltpu.make_async_remote_copy(
            src_ref=sbuf.at[peer],
            dst_ref=rbuf.at[dist],
            send_sem=send2_sem.at[dist],
            recv_sem=recv2_sem.at[dist],
            device_id=(peer, feat),
            device_id_type=MESH,
        )

    pl.semaphore_wait(all_in, n_x - 1)
    for dist in range(1, n_rows):
        exchange(dist).start()
    total = sbuf[row]
    for dist in range(1, n_rows):
        exchange(dist).wait_recv()
        total += rbuf[dist]

    width = n_elect * BINS
    bin_of = lax.rem(lax.broadcasted_iota(jnp.int32, total.shape, 1), BINS)
    left = total
    every = total
    shift = 1
    while shift < BINS:
        left += jnp.where(bin_of >= shift, pltpu.roll(left, shift, 1), 0.0)
        every += jnp.where(
            lax.rem(bin_of, 2 * shift) < shift,
            pltpu.roll(every, width - shift, 1),
            pltpu.roll(every, shift, 1),
        )
        shift *= 2
    right = every - left
    left_g, left_h = left[:own], left[own:]
    right_g, right_h = right[:own], right[own:]
    tot_g, tot_h = every[:own], every[own:]
    gains = 0.5 * (
        left_g * left_g / (left_h + l2_penalty)
        + right_g * right_g / (right_h + l2_penalty)
        - tot_g * tot_g / (tot_h + l2_penalty)
    )
    for e in range(n_elect):
        part = gains[:, (e // 2) * LANES : (e // 2 + 1) * LANES]
        if e % 2:
            part = pltpu.roll(part, BINS, 1)
        for c in range(own):
            out_ref[c, e : e + 1, :] = part[c : c + 1, : BINS - 1]

    for copy in own_sends:
        copy.wait_send()
    for slot in range(12, 28):
        send(feat, 0, other, slot, 0).wait_send()
    for dist in range(1, n_rows):
        exchange(dist).wait_send()


def shards(scores, labels, bins, elected):
    n_rows, n_feat = lax.axis_size("rows"), lax.axis_size("feat")
    own_rows, classes = scores.shape
    fgrp, rows = bins.shape
    n_elect = elected.shape[1]
    sub = own_rows // 4
    own = classes // n_rows
    n_x = math.gcd(n_rows, X_CHIPS)
    dma = pltpu.SemaphoreType.DMA
    return pl.pallas_call(
        functools.partial(kernel, n_rows, n_x, n_feat),
        out_shape=jax.ShapeDtypeStruct((own, n_elect, BINS - 1), jnp.float32),
        in_specs=[pl.BlockSpec(memory_space=pl.ANY)] * 4,
        out_specs=pl.BlockSpec(memory_space=pltpu.VMEM),
        scratch_shapes=[
            pltpu.VMEM((4, classes, sub), f32),
            pltpu.VMEM((rows // LANES, LANES), jnp.int32),
            pltpu.VMEM((UNITS, fgrp, 2 * sub), jnp.int32),
            pltpu.VMEM((n_elect, classes), jnp.int32),
            pltpu.VMEM((n_feat, 4, classes, sub), bf16),
            pltpu.VMEM((2 * classes, 2 * sub), bf16),
            pltpu.VMEM((2 * classes, fgrp * BINS), f32),
            pltpu.VMEM((n_rows, 2 * own, n_elect * BINS), f32),
            pltpu.VMEM((n_rows, 2 * own, n_elect * BINS), f32),
            dma((6,)),
            dma((PIECES,)),
            dma((28,)),
            dma((PIECES,)),
            dma((n_rows,)),
            dma((n_rows,)),
            pltpu.SemaphoreType.REGULAR,
        ],
        compiler_params=pltpu.CompilerParams(
            collective_id=0, has_side_effects=True, vmem_limit_bytes=60 << 20
        ),
    )(scores.T, labels.reshape(rows // LANES, LANES), bins, elected.T)


def solution(mesh):
    return jax.shard_map(
        shards,
        mesh=mesh,
        in_specs=(P(("rows", "feat"), None), P("rows"), P("feat", "rows"), P(None, "feat")),
        out_specs=P("rows", "feat", None),
        check_vma=False,
    )
```

```python
import functools
import math

import jax
import jax.numpy as jnp
from jax import lax
from jax.experimental import pallas as pl
from jax.experimental.pallas import tpu as pltpu
from jax.sharding import PartitionSpec as P

BINS = 64
LANES = 128
GROUP = 4
PIECES = 32
UNITS = PIECES // 2
X_CHIPS = 4
BLOCK = 256
MESH = pl.DeviceIdType.MESH
bf16 = jnp.bfloat16
f8 = jnp.float8_e4m3fn
f32 = jnp.float32

l2_penalty = 1.0


def code_probs(scores):
    expon = jnp.exp(scores - jnp.max(scores, axis=0, keepdims=True))
    probs = expon * (1.0 / jnp.sum(expon, axis=0, keepdims=True))
    return jnp.where(probs > 0.5, jnp.minimum(probs - 1.0, -1e-30), probs).astype(bf16)


def grad_hess(coded, is_label):
    zero, one = jnp.zeros((), bf16), jnp.ones((), bf16)
    shift = jnp.where(coded < zero, one, zero) - jnp.where(is_label, one, zero)
    size = jnp.abs(coded)
    return coded + shift, size * (one - size)


def kernel(
    n_rows,
    n_x,
    n_feat,
    scores_hbm,
    labels_hbm,
    bins_hbm,
    elected_hbm,
    out_ref,
    scores,
    labels,
    bins,
    elected,
    coded,
    gh,
    acc,
    chosen,
    picked,
    sbuf,
    rbuf,
    in_sem,
    bins_sem,
    send_sem,
    recv_sem,
    send2_sem,
    recv2_sem,
    all_in,
):
    n_y, n_z = n_feat // 2, n_rows // n_x
    row = lax.axis_index("rows")
    feat = lax.axis_index("feat")
    y, core = feat // 2, feat % 2
    z, x = row // n_x, row % n_x
    other = y * 2 + 1 - core
    plus = lax.rem(y + 1, n_y) * 2 + core
    minus = lax.rem(y + n_y - 1, n_y) * 2 + core
    sub = coded.shape[3]
    classes = coded.shape[2]
    fgrp = bins.shape[1]

    barrier = pltpu.get_barrier_semaphore()
    for peer in (other, plus, minus):
        pl.semaphore_signal(barrier, inc=1, device_id=(row, peer), device_id_type=MESH)
    for dist in range(1, n_x):
        peer = z * n_x + lax.rem(x + dist, n_x)
        pl.semaphore_signal(barrier, inc=1, device_id=(peer, feat), device_id_type=MESH)
    for dist in range(1, n_z):
        peer = lax.rem(z + dist, n_z) * n_x + x
        pl.semaphore_signal(barrier, inc=1, device_id=(peer, feat), device_id_type=MESH)

    def source(index):
        stage, kind = index // 4, lax.rem(index, 4)
        back = jnp.where(stage < 6, 1, 2)
        side = lax.rem(kind, 2)
        from_y = lax.rem(jnp.where(side == 0, y + n_y - back, y + back), n_y)
        from_core = jnp.where(kind < 2, core, 1 - core)
        near = jnp.where(stage == 0, feat, other)
        src = jnp.where(stage < 2, near, from_y * 2 + from_core)
        nth = jnp.where(stage < 2, kind // 2, jnp.where(stage < 6, stage - 2, stage - 6))
        return src, jnp.where(side == 0, nth, 3 - nth)

    def bins_copy(unit, side):
        src, quarter = source(2 * unit + side)
        start = pl.multiple_of((src * 4 + quarter) * sub, sub)
        return pltpu.make_async_copy(
            bins_hbm.at[:, pl.ds(start, sub)],
            bins.at[unit, :, pl.ds(side * sub, sub)],
            bins_sem.at[2 * unit + side],
        )

    own_order = (0, 3, 1, 2)
    copies = [
        pltpu.make_async_copy(
            scores_hbm.at[:, pl.ds(quarter * sub, sub)], scores.at[quarter], in_sem.at[quarter]
        )
        for quarter in own_order
    ]
    small = [
        pltpu.make_async_copy(labels_hbm, labels, in_sem.at[4]),
        pltpu.make_async_copy(elected_hbm, elected, in_sem.at[5]),
    ]
    for copy in copies + small:
        copy.start()

    def start_bins(unit, carry):
        bins_copy(unit, 0).start()
        bins_copy(unit, 1).start()
        return carry

    lax.fori_loop(0, UNITS, start_bins, 0)

    for quarter, copy in zip(own_order, copies):
        copy.wait()
        for lane in range(0, sub, BLOCK):
            lanes = slice(lane, min(lane + BLOCK, sub))
            coded[feat, quarter, :, lanes] = code_probs(scores[quarter, :, lanes])

    def send(src, quarter, peer, send_slot, recv_slot):
        return pltpu.make_async_remote_copy(
            src_ref=coded.at[src, quarter],
            dst_ref=coded.at[src, quarter],
            send_sem=send_sem.at[send_slot],
            recv_sem=recv_sem.at[recv_slot],
            device_id=(row, peer),
            device_id_type=MESH,
        )

    own_sends = []
    for nth in range(4):
        own_sends.append(send(feat, nth, plus, nth, 8 + 4 * nth))
        own_sends.append(send(feat, 3 - nth, minus, 4 + nth, 9 + 4 * nth))
        own_sends.append(send(feat, own_order[nth], other, 8 + nth, 4 + nth))

    acc[...] = jnp.zeros_like(acc)

    class_ids = lax.broadcasted_iota(jnp.int32, (classes, LANES), 0).astype(f32).astype(bf16)

    def receive(unit):
        stage, kind = unit // 2, 2 * lax.rem(unit, 2)
        pieces = [source(2 * unit + side) for side in range(2)]
        for side in range(2):
            send(*pieces[side], other, 0, 2 * unit + side).wait_recv()

        @pl.when((stage > 1) & (kind == 0))
        def _():
            for side in range(2):
                slot = 8 + stage * 2 + side
                send(*pieces[side], other, slot, 2 * unit + side + 2).start()

        @pl.when(((stage == 2) | (stage == 3)) & (kind == 0))
        def _():
            for side, onward in enumerate((plus, minus)):
                slot = 20 + stage * 2 + side
                send(*pieces[side], onward, slot, 2 * unit + side + 16).start()

        for side in range(2):
            bins_copy(unit, side).wait()

    tiles = sub // LANES
    groups = fgrp // GROUP

    def decode(unit):
        for tile in range(2 * tiles):
            src, quarter = source(2 * unit + tile // tiles)
            first = pl.multiple_of((src * 4 + quarter) * tiles, tiles)
            label = labels[pl.ds(first + tile % tiles, 1), :].astype(f32)
            label = jnp.broadcast_to(label, (classes, LANES)).astype(bf16)
            column = tile % tiles * LANES
            grad, hess = grad_hess(
                coded[src, quarter, :, column : column + LANES], label == class_ids
            )
            lanes = slice(tile * LANES, (tile + 1) * LANES)
            gh[0:classes, lanes] = grad
            gh[classes : 2 * classes, lanes] = hess

    def select(group):
        for e in range(elected.shape[0]):
            total = picked[e]
            for tile in range(group * GROUP // 2, (group + 1) * GROUP // 2):
                lanes = slice(tile * LANES, (tile + 1) * LANES)
                total += jnp.where(chosen[e] == 2.0 * tile, acc[:, lanes], 0.0)
            picked[e] = total

    def add_unit(unit, last=False):
        decode(unit)
        values = gh[...]
        shape = (BINS, 2 * sub)
        bin_ids = lax.broadcasted_iota(jnp.int32, shape, 0).astype(jnp.int8)
        ones, zeros = jnp.ones(shape, f8), jnp.zeros(shape, f8)
        for group in range(groups):
            onehot = []
            for feature in range(group * GROUP, (group + 1) * GROUP):
                code = bins[unit, feature : feature + 1, :]
                code = jnp.broadcast_to(code, shape).astype(jnp.int8)
                onehot.append(jnp.where(code == bin_ids, ones, zeros))
            columns = slice(group * GROUP * BINS, (group + 1) * GROUP * BINS)
            acc[:, columns] += lax.dot_general(
                values,
                jnp.concatenate(onehot, axis=0),
                (((1,), (1,)), ((), ())),
                preferred_element_type=f32,
            )
            if last and group > 0:
                select(group - 1)
        if last:
            select(groups - 1)

    for copy in small:
        copy.wait()

    def own_unit(unit):
        bins_copy(unit, 0).wait()
        bins_copy(unit, 1).wait()
        add_unit(unit)

    n_elect = elected.shape[0]
    local = (elected[...] - feat * fgrp).astype(f32)
    eye = jnp.where(
        lax.broadcasted_iota(jnp.int32, (classes, classes), 0)
        == lax.broadcasted_iota(jnp.int32, (classes, classes), 1),
        1.0,
        0.0,
    ).astype(f32)
    lane_ids = lax.broadcasted_iota(jnp.int32, (2 * classes, LANES), 1)
    upper = jnp.where(lane_ids >= BINS, 1.0, 0.0).astype(f32)
    for e in range(n_elect):
        per_class = jnp.sum(eye * local[e : e + 1, :], axis=1, keepdims=True)
        chosen[e] = jnp.concatenate([per_class, per_class], axis=0) - upper
        picked[e] = jnp.zeros((2 * classes, LANES), f32)
    own = classes // n_rows

    pl.semaphore_wait(barrier, n_x + n_z + 1)
    for copy in own_sends:
        copy.start()
    for dist in range(1, n_x):
        peer = z * n_x + lax.rem(x + dist, n_x)
        pl.semaphore_signal(all_in, inc=1, device_id=(peer, feat), device_id_type=MESH)
    own_unit(0)
    own_unit(1)

    def next_unit(unit, carry):
        receive(unit)
        add_unit(unit)
        return carry

    lax.fori_loop(2, UNITS - 1, next_unit, 0)
    receive(UNITS - 1)
    add_unit(UNITS - 1, last=True)

    def exchange(pair, dist_z, dist_x):
        to_z, to_x = lax.rem(z + dist_z, n_z), lax.rem(x + dist_x, n_x)
        peer = to_z * n_x + to_x
        slot = dist_z * n_x + dist_x
        return pltpu.make_async_remote_copy(
            src_ref=sbuf.at[pair, peer],
            dst_ref=rbuf.at[pair, slot],
            send_sem=send2_sem.at[pair * n_rows + slot],
            recv_sem=recv2_sem.at[pair * n_rows + slot],
            device_id=(peer, feat),
            device_id_type=MESH,
        )

    dists = [(dist_z, dist_x) for dist_z in range(n_z) for dist_x in range(n_x)][1:]
    dists.sort(key=lambda d: -min(d[0], n_z - d[0]) - min(d[1], n_x - d[1]))

    pl.semaphore_wait(all_in, n_x - 1)
    for pair in range(n_elect // 2):
        folded = [picked[e] + pltpu.roll(picked[e], BINS, 1) for e in (2 * pair, 2 * pair + 1)]
        both = jnp.where(lane_ids < BINS, folded[0], folded[1])
        for owner in range(n_rows):
            sbuf[pair, owner, 0:own] = both[owner * own : (owner + 1) * own]
            sbuf[pair, owner, own : 2 * own] = both[
                classes + owner * own : classes + (owner + 1) * own
            ]
        for dist in dists:
            exchange(pair, *dist).start()
    totals = []
    for pair in range(n_elect // 2):
        total = sbuf[pair, row]
        for dist in reversed(dists):
            exchange(pair, *dist).wait_recv()
            total += rbuf[pair, dist[0] * n_x + dist[1]]
        totals.append(total)
    total = jnp.concatenate(totals, axis=1)

    width = n_elect * BINS
    bin_of = lax.rem(lax.broadcasted_iota(jnp.int32, total.shape, 1), BINS)
    left = total
    every = total
    shift = 1
    while shift < BINS:
        left += jnp.where(bin_of >= shift, pltpu.roll(left, shift, 1), 0.0)
        every += jnp.where(
            lax.rem(bin_of, 2 * shift) < shift,
            pltpu.roll(every, width - shift, 1),
            pltpu.roll(every, shift, 1),
        )
        shift *= 2
    right = every - left
    left_g, left_h = left[:own], left[own:]
    right_g, right_h = right[:own], right[own:]
    tot_g, tot_h = every[:own], every[own:]
    gains = 0.5 * (
        left_g * left_g / (left_h + l2_penalty)
        + right_g * right_g / (right_h + l2_penalty)
        - tot_g * tot_g / (tot_h + l2_penalty)
    )
    for e in range(n_elect):
        part = gains[:, (e // 2) * LANES : (e // 2 + 1) * LANES]
        if e % 2:
            part = pltpu.roll(part, BINS, 1)
        for c in range(own):
            out_ref[c, e : e + 1, :] = part[c : c + 1, : BINS - 1]

    for copy in own_sends:
        copy.wait_send()
    for slot in range(12, 28):
        send(feat, 0, other, slot, 0).wait_send()
    for pair in range(n_elect // 2):
        for dist in dists:
            exchange(pair, *dist).wait_send()


def shards(scores, labels, bins, elected):
    n_rows, n_feat = lax.axis_size("rows"), lax.axis_size("feat")
    own_rows, classes = scores.shape
    fgrp, rows = bins.shape
    n_elect = elected.shape[1]
    sub = own_rows // 4
    own = classes // n_rows
    n_x = math.gcd(n_rows, X_CHIPS)
    dma = pltpu.SemaphoreType.DMA
    return pl.pallas_call(
        functools.partial(kernel, n_rows, n_x, n_feat),
        out_shape=pltpu.VMEM((own, n_elect, BINS - 1), jnp.float32),
        in_specs=[pl.BlockSpec(memory_space=pl.ANY)] * 4,
        out_specs=pl.BlockSpec(memory_space=pltpu.VMEM),
        scratch_shapes=[
            pltpu.VMEM((4, classes, sub), f32),
            pltpu.VMEM((rows // LANES, LANES), jnp.int32),
            pltpu.VMEM((UNITS, fgrp, 2 * sub), jnp.int32),
            pltpu.VMEM((n_elect, classes), jnp.int32),
            pltpu.VMEM((n_feat, 4, classes, sub), bf16),
            pltpu.VMEM((2 * classes, 2 * sub), bf16),
            pltpu.VMEM((2 * classes, fgrp * BINS), f32),
            pltpu.VMEM((n_elect, 2 * classes, LANES), f32),
            pltpu.VMEM((n_elect, 2 * classes, LANES), f32),
            pltpu.VMEM((n_elect // 2, n_rows, 2 * own, LANES), f32),
            pltpu.VMEM((n_elect // 2, n_rows, 2 * own, LANES), f32),
            dma((6,)),
            dma((PIECES,)),
            dma((28,)),
            dma((PIECES,)),
            dma((n_elect // 2 * n_rows,)),
            dma((n_elect // 2 * n_rows,)),
            pltpu.SemaphoreType.REGULAR,
        ],
        compiler_params=pltpu.CompilerParams(
            collective_id=0, has_side_effects=True, vmem_limit_bytes=60 << 20
        ),
    )(scores.T, labels.reshape(rows // LANES, LANES), bins, elected.T)


def solution(mesh):
    return jax.shard_map(
        shards,
        mesh=mesh,
        in_specs=(P(("rows", "feat"), None), P("rows"), P("feat", "rows"), P(None, "feat")),
        out_specs=P("rows", "feat", None),
        check_vma=False,
    )
```

```python
import functools
import math

import jax
import jax.numpy as jnp
from jax import lax
from jax.experimental import pallas as pl
from jax.experimental.pallas import tpu as pltpu
from jax.sharding import PartitionSpec as P

BINS = 64
LANES = 128
GROUP = 4
PIECES = 32
UNITS = PIECES // 2
X_CHIPS = 4
BLOCK = 256
MESH = pl.DeviceIdType.MESH
bf16 = jnp.bfloat16
f8 = jnp.float8_e4m3fn
f32 = jnp.float32

l2_penalty = 1.0


def code_probs(scores):
    expon = jnp.exp(scores - jnp.max(scores, axis=0, keepdims=True))
    probs = expon * (1.0 / jnp.sum(expon, axis=0, keepdims=True))
    return jnp.where(probs > 0.5, jnp.minimum(probs - 1.0, -1e-30), probs).astype(bf16)


def grad_hess(coded, is_label):
    zero, one = jnp.zeros((), bf16), jnp.ones((), bf16)
    shift = jnp.where(coded < zero, one, zero) - jnp.where(is_label, one, zero)
    size = jnp.abs(coded)
    return coded + shift, size * (one - size)


def kernel(
    n_rows,
    n_x,
    n_feat,
    scores_hbm,
    labels_hbm,
    bins_hbm,
    elected_hbm,
    out_ref,
    scores,
    labels,
    bins,
    elected,
    coded,
    gh,
    acc,
    chosen,
    picked,
    sbuf,
    rbuf,
    in_sem,
    send_sem,
    recv_sem,
    send2_sem,
    recv2_sem,
    all_in,
):
    n_y, n_z = n_feat // 2, n_rows // n_x
    row = lax.axis_index("rows")
    feat = lax.axis_index("feat")
    y, core = feat // 2, feat % 2
    z, x = row // n_x, row % n_x
    other = y * 2 + 1 - core
    plus = lax.rem(y + 1, n_y) * 2 + core
    minus = lax.rem(y + n_y - 1, n_y) * 2 + core
    sub = coded.shape[3]
    classes = coded.shape[2]
    fgrp = bins.shape[0]

    barrier = pltpu.get_barrier_semaphore()
    for peer in (other, plus, minus):
        pl.semaphore_signal(barrier, inc=1, device_id=(row, peer), device_id_type=MESH)
    for dist in range(1, n_x):
        peer = z * n_x + lax.rem(x + dist, n_x)
        pl.semaphore_signal(barrier, inc=1, device_id=(peer, feat), device_id_type=MESH)
    for dist in range(1, n_z):
        peer = lax.rem(z + dist, n_z) * n_x + x
        pl.semaphore_signal(barrier, inc=1, device_id=(peer, feat), device_id_type=MESH)

    def source(index):
        stage, kind = index // 4, lax.rem(index, 4)
        back = jnp.where(stage < 6, 1, 2)
        side = lax.rem(kind, 2)
        from_y = lax.rem(jnp.where(side == 0, y + n_y - back, y + back), n_y)
        from_core = jnp.where(kind < 2, core, 1 - core)
        near = jnp.where(stage == 0, feat, other)
        src = jnp.where(stage < 2, near, from_y * 2 + from_core)
        nth = jnp.where(stage < 2, kind // 2, jnp.where(stage < 6, stage - 2, stage - 6))
        return src, jnp.where(side == 0, nth, 3 - nth)

    own_order = (0, 3, 1, 2)
    copies = [
        pltpu.make_async_copy(
            scores_hbm.at[:, pl.ds(quarter * sub, sub)], scores.at[quarter], in_sem.at[quarter]
        )
        for quarter in own_order
    ]
    small = [
        pltpu.make_async_copy(labels_hbm, labels, in_sem.at[4]),
        pltpu.make_async_copy(elected_hbm, elected, in_sem.at[5]),
        pltpu.make_async_copy(bins_hbm, bins, in_sem.at[6]),
    ]
    for copy in copies + small:
        copy.start()

    def code_own(nth):
        quarter = own_order[nth]
        copies[nth].wait()
        for lane in range(0, sub, BLOCK):
            lanes = slice(lane, min(lane + BLOCK, sub))
            coded[feat, quarter, :, lanes] = code_probs(scores[quarter, :, lanes])

    def send(src, quarter, peer, send_slot, recv_slot):
        return pltpu.make_async_remote_copy(
            src_ref=coded.at[src, quarter],
            dst_ref=coded.at[src, quarter],
            send_sem=send_sem.at[send_slot],
            recv_sem=recv_sem.at[recv_slot],
            device_id=(row, peer),
            device_id_type=MESH,
        )

    own_sends = [
        (
            send(feat, nth, plus, nth, 8 + 4 * nth),
            send(feat, 3 - nth, minus, 4 + nth, 9 + 4 * nth),
            send(feat, own_order[nth], other, 8 + nth, 4 + nth),
        )
        for nth in range(4)
    ]
    to_plus, to_minus, to_other = zip(*own_sends)
    code_own(0)
    code_own(1)
    pl.semaphore_wait(barrier, n_x + n_z + 1)
    for copy in (to_plus[0], to_minus[0], *to_other[:2]):
        copy.start()
    code_own(2)
    code_own(3)
    for copy in (to_plus[1], to_minus[1], to_plus[2], to_minus[2], to_plus[3], to_minus[3]):
        copy.start()
    for copy in to_other[2:]:
        copy.start()
    for dist in range(1, n_x):
        peer = z * n_x + lax.rem(x + dist, n_x)
        pl.semaphore_signal(all_in, inc=1, device_id=(peer, feat), device_id_type=MESH)
    acc[...] = jnp.zeros_like(acc)

    class_ids = lax.broadcasted_iota(jnp.int32, (classes, LANES), 0).astype(f32).astype(bf16)

    def receive(unit):
        stage, kind = unit // 2, 2 * lax.rem(unit, 2)
        pieces = [source(2 * unit + side) for side in range(2)]
        for side in range(2):
            send(*pieces[side], other, 0, 2 * unit + side).wait_recv()

        @pl.when((stage > 1) & (kind == 0))
        def _():
            for side in range(2):
                slot = 8 + stage * 2 + side
                send(*pieces[side], other, slot, 2 * unit + side + 2).start()

        @pl.when(((stage == 2) | (stage == 3)) & (kind == 0))
        def _():
            for side, onward in enumerate((plus, minus)):
                slot = 20 + stage * 2 + side
                send(*pieces[side], onward, slot, 2 * unit + side + 16).start()

    tiles = sub // LANES
    groups = fgrp // GROUP

    def decode(unit):
        for tile in range(2 * tiles):
            src, quarter = source(2 * unit + tile // tiles)
            first = pl.multiple_of((src * 4 + quarter) * tiles, tiles)
            label = labels[pl.ds(first + tile % tiles, 1), :].astype(f32)
            label = jnp.broadcast_to(label, (classes, LANES)).astype(bf16)
            column = tile % tiles * LANES
            grad, hess = grad_hess(
                coded[src, quarter, :, column : column + LANES], label == class_ids
            )
            lanes = slice(tile * LANES, (tile + 1) * LANES)
            gh[0:classes, lanes] = grad
            gh[classes : 2 * classes, lanes] = hess

    def select(group):
        for e in range(elected.shape[0]):
            total = picked[e]
            for tile in range(group * GROUP // 2, (group + 1) * GROUP // 2):
                lanes = slice(tile * LANES, (tile + 1) * LANES)
                total += jnp.where(chosen[e] == 2.0 * tile, acc[:, lanes], 0.0)
            picked[e] = total

    def add_unit(unit, last=False):
        decode(unit)
        values = gh[...]
        pieces = [source(2 * unit + side) for side in range(2)]
        starts = [pl.multiple_of((src * 4 + quarter) * sub, sub) for src, quarter in pieces]
        shape = (BINS, 2 * sub)
        bin_ids = lax.broadcasted_iota(jnp.int32, shape, 0).astype(jnp.int8)
        ones, zeros = jnp.ones(shape, f8), jnp.zeros(shape, f8)
        for group in range(groups):
            onehot = []
            for feature in range(group * GROUP, (group + 1) * GROUP):
                code = jnp.concatenate(
                    [bins[feature : feature + 1, pl.ds(start, sub)] for start in starts], axis=1
                )
                code = jnp.broadcast_to(code, shape).astype(jnp.int8)
                onehot.append(jnp.where(code == bin_ids, ones, zeros))
            columns = slice(group * GROUP * BINS, (group + 1) * GROUP * BINS)
            acc[:, columns] += lax.dot_general(
                values,
                jnp.concatenate(onehot, axis=0),
                (((1,), (1,)), ((), ())),
                preferred_element_type=f32,
            )
            if last and group > 0:
                select(group - 1)
        if last:
            select(groups - 1)

    for copy in small:
        copy.wait()

    n_elect = elected.shape[0]
    local = (elected[...] - feat * fgrp).astype(f32)
    eye = jnp.where(
        lax.broadcasted_iota(jnp.int32, (classes, classes), 0)
        == lax.broadcasted_iota(jnp.int32, (classes, classes), 1),
        1.0,
        0.0,
    ).astype(f32)
    lane_ids = lax.broadcasted_iota(jnp.int32, (2 * classes, LANES), 1)
    upper = jnp.where(lane_ids >= BINS, 1.0, 0.0).astype(f32)
    for e in range(n_elect):
        per_class = jnp.sum(eye * local[e : e + 1, :], axis=1, keepdims=True)
        chosen[e] = jnp.concatenate([per_class, per_class], axis=0) - upper
        picked[e] = jnp.zeros((2 * classes, LANES), f32)
    own = classes // n_rows

    add_unit(0)
    add_unit(1)

    def next_unit(unit, carry):
        receive(unit)
        add_unit(unit)
        return carry

    lax.fori_loop(2, UNITS - 1, next_unit, 0)
    receive(UNITS - 1)
    add_unit(UNITS - 1, last=True)

    def exchange(pair, dist_z, dist_x):
        to_z, to_x = lax.rem(z + dist_z, n_z), lax.rem(x + dist_x, n_x)
        peer = to_z * n_x + to_x
        slot = dist_z * n_x + dist_x
        return pltpu.make_async_remote_copy(
            src_ref=sbuf.at[pair, peer],
            dst_ref=rbuf.at[pair, slot],
            send_sem=send2_sem.at[pair * n_rows + slot],
            recv_sem=recv2_sem.at[pair * n_rows + slot],
            device_id=(peer, feat),
            device_id_type=MESH,
        )

    dists = [(dist_z, dist_x) for dist_z in range(n_z) for dist_x in range(n_x)][1:]
    dists.sort(key=lambda d: -min(d[0], n_z - d[0]) - min(d[1], n_x - d[1]))

    pl.semaphore_wait(all_in, n_x - 1)
    for pair in range(n_elect // 2):
        folded = [picked[e] + pltpu.roll(picked[e], BINS, 1) for e in (2 * pair, 2 * pair + 1)]
        both = jnp.where(lane_ids < BINS, folded[0], folded[1])
        for owner in range(n_rows):
            sbuf[pair, owner, 0:own] = both[owner * own : (owner + 1) * own]
            sbuf[pair, owner, own : 2 * own] = both[
                classes + owner * own : classes + (owner + 1) * own
            ]
        for dist in dists:
            exchange(pair, *dist).start()
    totals = []
    for pair in range(n_elect // 2):
        total = sbuf[pair, row]
        for dist in reversed(dists):
            exchange(pair, *dist).wait_recv()
            total += rbuf[pair, dist[0] * n_x + dist[1]]
        totals.append(total)
    total = jnp.concatenate(totals, axis=1)

    width = n_elect * BINS
    bin_of = lax.rem(lax.broadcasted_iota(jnp.int32, total.shape, 1), BINS)
    left = total
    every = total
    shift = 1
    while shift < BINS:
        left += jnp.where(bin_of >= shift, pltpu.roll(left, shift, 1), 0.0)
        every += jnp.where(
            lax.rem(bin_of, 2 * shift) < shift,
            pltpu.roll(every, width - shift, 1),
            pltpu.roll(every, shift, 1),
        )
        shift *= 2
    right = every - left
    left_g, left_h = left[:own], left[own:]
    right_g, right_h = right[:own], right[own:]
    tot_g, tot_h = every[:own], every[own:]
    gains = 0.5 * (
        left_g * left_g / (left_h + l2_penalty)
        + right_g * right_g / (right_h + l2_penalty)
        - tot_g * tot_g / (tot_h + l2_penalty)
    )
    for e in range(n_elect):
        part = gains[:, (e // 2) * LANES : (e // 2 + 1) * LANES]
        if e % 2:
            part = pltpu.roll(part, BINS, 1)
        for c in range(own):
            out_ref[c, e : e + 1, :] = part[c : c + 1, : BINS - 1]

    for copy in to_plus + to_minus + to_other:
        copy.wait_send()
    for slot in range(12, 28):
        send(feat, 0, other, slot, 0).wait_send()
    for pair in range(n_elect // 2):
        for dist in dists:
            exchange(pair, *dist).wait_send()


def shards(scores, labels, bins, elected):
    n_rows, n_feat = lax.axis_size("rows"), lax.axis_size("feat")
    own_rows, classes = scores.shape
    fgrp, rows = bins.shape
    n_elect = elected.shape[1]
    sub = own_rows // 4
    own = classes // n_rows
    n_x = math.gcd(n_rows, X_CHIPS)
    dma = pltpu.SemaphoreType.DMA
    return pl.pallas_call(
        functools.partial(kernel, n_rows, n_x, n_feat),
        out_shape=pltpu.VMEM((own, n_elect, BINS - 1), jnp.float32),
        in_specs=[pl.BlockSpec(memory_space=pl.ANY)] * 4,
        out_specs=pl.BlockSpec(memory_space=pltpu.VMEM),
        scratch_shapes=[
            pltpu.VMEM((4, classes, sub), f32),
            pltpu.VMEM((rows // LANES, LANES), jnp.int32),
            pltpu.VMEM((fgrp, rows), jnp.int32),
            pltpu.VMEM((n_elect, classes), jnp.int32),
            pltpu.VMEM((n_feat, 4, classes, sub), bf16),
            pltpu.VMEM((2 * classes, 2 * sub), bf16),
            pltpu.VMEM((2 * classes, fgrp * BINS), f32),
            pltpu.VMEM((n_elect, 2 * classes, LANES), f32),
            pltpu.VMEM((n_elect, 2 * classes, LANES), f32),
            pltpu.VMEM((n_elect // 2, n_rows, 2 * own, LANES), f32),
            pltpu.VMEM((n_elect // 2, n_rows, 2 * own, LANES), f32),
            dma((7,)),
            dma((28,)),
            dma((PIECES,)),
            dma((n_elect // 2 * n_rows,)),
            dma((n_elect // 2 * n_rows,)),
            pltpu.SemaphoreType.REGULAR,
        ],
        compiler_params=pltpu.CompilerParams(
            collective_id=0, has_side_effects=True, vmem_limit_bytes=60 << 20
        ),
    )(scores.T, labels.reshape(rows // LANES, LANES), bins, elected.T)


def solution(mesh):
    return jax.shard_map(
        shards,
        mesh=mesh,
        in_specs=(P(("rows", "feat"), None), P("rows"), P("feat", "rows"), P(None, "feat")),
        out_specs=P("rows", "feat", None),
        check_vma=False,
    )
```

```python
import functools
import math

import jax
import jax.numpy as jnp
from jax import lax
from jax.experimental import pallas as pl
from jax.experimental.pallas import tpu as pltpu
from jax.sharding import PartitionSpec as P

BINS = 64
LANES = 128
GROUP = 4
PIECES = 32
UNITS = PIECES // 2
X_CHIPS = 4
BLOCK = 256
MESH = pl.DeviceIdType.MESH
bf16 = jnp.bfloat16
f8 = jnp.float8_e4m3fn
f32 = jnp.float32

l2_penalty = 1.0


def code_probs(scores):
    expon = jnp.exp(scores - jnp.max(scores, axis=0, keepdims=True))
    probs = expon * (1.0 / jnp.sum(expon, axis=0, keepdims=True))
    return jnp.where(probs > 0.5, jnp.minimum(probs - 1.0, -1e-30), probs).astype(bf16)


def grad_hess(coded, is_label):
    zero, one = jnp.zeros((), bf16), jnp.ones((), bf16)
    shift = jnp.where(coded < zero, one, zero) - jnp.where(is_label, one, zero)
    size = jnp.abs(coded)
    return coded + shift, size * (one - size)


def kernel(
    n_rows,
    n_x,
    n_feat,
    scores_hbm,
    labels_hbm,
    bins_hbm,
    elected_hbm,
    out_ref,
    scores,
    labels,
    bins,
    elected,
    coded,
    gh,
    acc,
    chosen,
    picked,
    sbuf,
    rbuf,
    in_sem,
    send_sem,
    recv_sem,
    send2_sem,
    recv2_sem,
    all_in,
):
    n_y, n_z = n_feat // 2, n_rows // n_x
    row = lax.axis_index("rows")
    feat = lax.axis_index("feat")
    y, core = feat // 2, feat % 2
    z, x = row // n_x, row % n_x
    other = y * 2 + 1 - core
    plus = lax.rem(y + 1, n_y) * 2 + core
    minus = lax.rem(y + n_y - 1, n_y) * 2 + core
    sub = coded.shape[3]
    classes = coded.shape[2]
    fgrp = bins.shape[0]

    barrier = pltpu.get_barrier_semaphore()
    for peer in (other, plus, minus):
        pl.semaphore_signal(barrier, inc=1, device_id=(row, peer), device_id_type=MESH)
    for dist in range(1, n_x):
        peer = z * n_x + lax.rem(x + dist, n_x)
        pl.semaphore_signal(barrier, inc=1, device_id=(peer, feat), device_id_type=MESH)
    for dist in range(1, n_z):
        peer = lax.rem(z + dist, n_z) * n_x + x
        pl.semaphore_signal(barrier, inc=1, device_id=(peer, feat), device_id_type=MESH)

    def source(index):
        stage, kind = index // 4, lax.rem(index, 4)
        back = jnp.where(stage < 6, 1, 2)
        side = lax.rem(kind, 2)
        from_y = lax.rem(jnp.where(side == 0, y + n_y - back, y + back), n_y)
        from_core = jnp.where(kind < 2, core, 1 - core)
        near = jnp.where(stage == 0, feat, other)
        src = jnp.where(stage < 2, near, from_y * 2 + from_core)
        nth = jnp.where(stage < 2, kind // 2, jnp.where(stage < 6, stage - 2, stage - 6))
        return src, jnp.where(side == 0, nth, 3 - nth)

    own_order = (0, 3, 1, 2)
    copies = [
        pltpu.make_async_copy(
            scores_hbm.at[:, pl.ds(quarter * sub, sub)], scores.at[quarter], in_sem.at[quarter]
        )
        for quarter in own_order
    ]
    small = [
        pltpu.make_async_copy(labels_hbm, labels, in_sem.at[4]),
        pltpu.make_async_copy(elected_hbm, elected, in_sem.at[5]),
        pltpu.make_async_copy(bins_hbm, bins, in_sem.at[6]),
    ]
    for copy in copies + small:
        copy.start()

    def code_own(nth):
        quarter = own_order[nth]
        copies[nth].wait()
        for lane in range(0, sub, BLOCK):
            lanes = slice(lane, min(lane + BLOCK, sub))
            coded[feat, quarter, :, lanes] = code_probs(scores[quarter, :, lanes])

    def send(src, quarter, peer, send_slot, recv_slot):
        return pltpu.make_async_remote_copy(
            src_ref=coded.at[src, quarter],
            dst_ref=coded.at[src, quarter],
            send_sem=send_sem.at[send_slot],
            recv_sem=recv_sem.at[recv_slot],
            device_id=(row, peer),
            device_id_type=MESH,
        )

    own_sends = [
        (
            send(feat, nth, plus, nth, 8 + 4 * nth),
            send(feat, 3 - nth, minus, 4 + nth, 9 + 4 * nth),
            send(feat, own_order[nth], other, 8 + nth, 4 + nth),
        )
        for nth in range(4)
    ]
    to_plus, to_minus, to_other = zip(*own_sends)
    code_own(0)
    code_own(1)
    pl.semaphore_wait(barrier, n_x + n_z + 1)
    for copy in (to_plus[0], to_minus[0], *to_other[:2]):
        copy.start()
    code_own(2)
    code_own(3)
    for copy in (to_plus[1], to_minus[1], to_plus[2], to_minus[2], to_plus[3], to_minus[3]):
        copy.start()
    for copy in to_other[2:]:
        copy.start()
    for dist in range(1, n_x):
        peer = z * n_x + lax.rem(x + dist, n_x)
        pl.semaphore_signal(all_in, inc=1, device_id=(peer, feat), device_id_type=MESH)
    acc[...] = jnp.zeros_like(acc)

    class_ids = lax.broadcasted_iota(jnp.int32, (classes, LANES), 0).astype(f32).astype(bf16)

    def receive(unit):
        stage, kind = unit // 2, 2 * lax.rem(unit, 2)
        pieces = [source(2 * unit + side) for side in range(2)]
        for side in range(2):
            send(*pieces[side], other, 0, 2 * unit + side).wait_recv()

        @pl.when((stage > 1) & (kind == 0))
        def _():
            for side in range(2):
                slot = 8 + stage * 2 + side
                send(*pieces[side], other, slot, 2 * unit + side + 2).start()

        @pl.when(((stage == 2) | (stage == 3)) & (kind == 0))
        def _():
            for side, onward in enumerate((plus, minus)):
                slot = 20 + stage * 2 + side
                send(*pieces[side], onward, slot, 2 * unit + side + 16).start()

    tiles = sub // LANES
    groups = fgrp // GROUP

    def decode(unit):
        for tile in range(2 * tiles):
            src, quarter = source(2 * unit + tile // tiles)
            first = pl.multiple_of((src * 4 + quarter) * tiles, tiles)
            label = labels[pl.ds(first + tile % tiles, 1), :].astype(f32)
            label = jnp.broadcast_to(label, (classes, LANES)).astype(bf16)
            column = tile % tiles * LANES
            grad, hess = grad_hess(
                coded[src, quarter, :, column : column + LANES], label == class_ids
            )
            lanes = slice(tile * LANES, (tile + 1) * LANES)
            gh[0:classes, lanes] = grad
            gh[classes : 2 * classes, lanes] = hess

    def select(group):
        for e in range(elected.shape[0]):
            total = picked[e]
            for tile in range(group * GROUP // 2, (group + 1) * GROUP // 2):
                lanes = slice(tile * LANES, (tile + 1) * LANES)
                total += jnp.where(chosen[e] == 2.0 * tile, acc[:, lanes], 0.0)
            picked[e] = total

    def add_unit(unit, last=False):
        decode(unit)
        values = gh[...]
        pieces = [source(2 * unit + side) for side in range(2)]
        starts = [pl.multiple_of((src * 4 + quarter) * sub, sub) for src, quarter in pieces]
        shape = (BINS, 2 * sub)
        bin_ids = lax.broadcasted_iota(jnp.int32, shape, 0).astype(jnp.int8)
        ones, zeros = jnp.ones(shape, f8), jnp.zeros(shape, f8)
        for group in range(groups):
            onehot = []
            for feature in range(group * GROUP, (group + 1) * GROUP):
                code = jnp.concatenate(
                    [bins[feature : feature + 1, pl.ds(start, sub)] for start in starts], axis=1
                )
                code = jnp.broadcast_to(code, shape).astype(jnp.int8)
                onehot.append(jnp.where(code == bin_ids, ones, zeros))
            columns = slice(group * GROUP * BINS, (group + 1) * GROUP * BINS)
            acc[:, columns] += lax.dot_general(
                values,
                jnp.concatenate(onehot, axis=0),
                (((1,), (1,)), ((), ())),
                preferred_element_type=f32,
            )
            if last and group > 0:
                select(group - 1)
        if last:
            select(groups - 1)

    for copy in small:
        copy.wait()

    n_elect = elected.shape[0]
    local = (elected[...] - feat * fgrp).astype(f32)
    eye = jnp.where(
        lax.broadcasted_iota(jnp.int32, (classes, classes), 0)
        == lax.broadcasted_iota(jnp.int32, (classes, classes), 1),
        1.0,
        0.0,
    ).astype(f32)
    lane_ids = lax.broadcasted_iota(jnp.int32, (2 * classes, LANES), 1)
    upper = jnp.where(lane_ids >= BINS, 1.0, 0.0).astype(f32)
    for e in range(n_elect):
        per_class = jnp.sum(eye * local[e : e + 1, :], axis=1, keepdims=True)
        chosen[e] = jnp.concatenate([per_class, per_class], axis=0) - upper
        picked[e] = jnp.zeros((2 * classes, LANES), f32)
    own = classes // n_rows

    add_unit(0)
    add_unit(1)

    def next_unit(unit, carry):
        receive(unit)
        add_unit(unit)
        return carry

    lax.fori_loop(2, UNITS - 1, next_unit, 0)
    receive(UNITS - 1)
    add_unit(UNITS - 1, last=True)

    def exchange(dist_z, dist_x):
        to_z, to_x = lax.rem(z + dist_z, n_z), lax.rem(x + dist_x, n_x)
        peer = to_z * n_x + to_x
        slot = dist_z * n_x + dist_x
        return pltpu.make_async_remote_copy(
            src_ref=sbuf.at[peer],
            dst_ref=rbuf.at[slot],
            send_sem=send2_sem.at[slot],
            recv_sem=recv2_sem.at[slot],
            device_id=(peer, feat),
            device_id_type=MESH,
        )

    dists = [(dist_z, dist_x) for dist_z in range(n_z) for dist_x in range(n_x)][1:]
    dists.sort(key=lambda d: -min(d[0], n_z - d[0]) - min(d[1], n_x - d[1]))

    for pair in range(n_elect // 2):
        folded = [picked[e] + pltpu.roll(picked[e], BINS, 1) for e in (2 * pair, 2 * pair + 1)]
        both = jnp.where(lane_ids < BINS, folded[0], folded[1])
        columns = slice(pair * LANES, (pair + 1) * LANES)
        for owner in range(n_rows):
            sbuf[owner, 0:own, columns] = both[owner * own : (owner + 1) * own]
            sbuf[owner, own : 2 * own, columns] = both[
                classes + owner * own : classes + (owner + 1) * own
            ]
    pl.semaphore_wait(all_in, n_x - 1)
    for dist in dists:
        exchange(*dist).start()
    total = sbuf[row]
    for dist in reversed(dists):
        exchange(*dist).wait_recv()
        total += rbuf[dist[0] * n_x + dist[1]]

    width = n_elect * BINS
    bin_of = lax.rem(lax.broadcasted_iota(jnp.int32, total.shape, 1), BINS)
    left = total
    every = total
    shift = 1
    while shift < BINS:
        left += jnp.where(bin_of >= shift, pltpu.roll(left, shift, 1), 0.0)
        every += jnp.where(
            lax.rem(bin_of, 2 * shift) < shift,
            pltpu.roll(every, width - shift, 1),
            pltpu.roll(every, shift, 1),
        )
        shift *= 2
    right = every - left
    left_g, left_h = left[:own], left[own:]
    right_g, right_h = right[:own], right[own:]
    tot_g, tot_h = every[:own], every[own:]
    gains = 0.5 * (
        left_g * left_g / (left_h + l2_penalty)
        + right_g * right_g / (right_h + l2_penalty)
        - tot_g * tot_g / (tot_h + l2_penalty)
    )
    for e in range(n_elect):
        part = gains[:, (e // 2) * LANES : (e // 2 + 1) * LANES]
        if e % 2:
            part = pltpu.roll(part, BINS, 1)
        for c in range(own):
            out_ref[c, e : e + 1, :] = part[c : c + 1, : BINS - 1]

    for copy in to_plus + to_minus + to_other:
        copy.wait_send()
    for slot in range(12, 28):
        send(feat, 0, other, slot, 0).wait_send()
    for dist in dists:
        exchange(*dist).wait_send()


def shards(scores, labels, bins, elected):
    n_rows, n_feat = lax.axis_size("rows"), lax.axis_size("feat")
    own_rows, classes = scores.shape
    fgrp, rows = bins.shape
    n_elect = elected.shape[1]
    sub = own_rows // 4
    own = classes // n_rows
    n_x = math.gcd(n_rows, X_CHIPS)
    dma = pltpu.SemaphoreType.DMA
    return pl.pallas_call(
        functools.partial(kernel, n_rows, n_x, n_feat),
        out_shape=pltpu.VMEM((own, n_elect, BINS - 1), jnp.float32),
        in_specs=[pl.BlockSpec(memory_space=pl.ANY)] * 4,
        out_specs=pl.BlockSpec(memory_space=pltpu.VMEM),
        scratch_shapes=[
            pltpu.VMEM((4, classes, sub), f32),
            pltpu.VMEM((rows // LANES, LANES), jnp.int32),
            pltpu.VMEM((fgrp, rows), jnp.int32),
            pltpu.VMEM((n_elect, classes), jnp.int32),
            pltpu.VMEM((n_feat, 4, classes, sub), bf16),
            pltpu.VMEM((2 * classes, 2 * sub), bf16),
            pltpu.VMEM((2 * classes, fgrp * BINS), f32),
            pltpu.VMEM((n_elect, 2 * classes, LANES), f32),
            pltpu.VMEM((n_elect, 2 * classes, LANES), f32),
            pltpu.VMEM((n_rows, 2 * own, n_elect * BINS), f32),
            pltpu.VMEM((n_rows, 2 * own, n_elect * BINS), f32),
            dma((7,)),
            dma((28,)),
            dma((PIECES,)),
            dma((n_rows,)),
            dma((n_rows,)),
            pltpu.SemaphoreType.REGULAR,
        ],
        compiler_params=pltpu.CompilerParams(
            collective_id=0, has_side_effects=True, vmem_limit_bytes=60 << 20
        ),
    )(scores.T, labels.reshape(rows // LANES, LANES), bins, elected.T)


def solution(mesh):
    return jax.shard_map(
        shards,
        mesh=mesh,
        in_specs=(P(("rows", "feat"), None), P("rows"), P("feat", "rows"), P(None, "feat")),
        out_specs=P("rows", "feat", None),
        check_vma=False,
    )
```
